256 devices in a mesh: samp: 4 (over y), var: 64 (over z, x, core).
Axes of the slice: x: 4, y: 4, z: 8, core: 2. Of those that a mesh axis runs over, the one named last changes fastest.
Arguments:
- dosage: bfloat16 [8192, 131072], P('samp', 'var'), may hold values from -16 to 16
- traits: float32 [8192, 128], P(('samp', 'var')), may hold values from -6 to 6
- coef_now: float32 [1024, 256, 128], P('var', 'samp'), may hold values from -6 to 6
- coef_prev: float32 [1024, 256, 128], P('var', 'samp'), may hold values from -6 to 6
- block_inverse: bfloat16 [1024, 256, 4, 256], P('var', 'samp'), may hold values from -0.1875 to 0.1875
- penalty: float32 [128], replicated, may hold values from 0.05 to 0.5
- block_start: int32 [512], replicated, may hold values from 0 to 1, as said below
- unit_owner: int32 [512], replicated, may hold values from 0 to 63, as said below
Outputs:
- coef_next: float32 [1024, 256, 128], P('var', 'samp')
- residual: float32 [8192, 128], P(('samp', 'var'))
The draws below stay inside these ranges and needn't reach their ends.
Inputs may be any that keep to these rules, and one draw needn't show every extreme that they name: `block_start`: 1 where a linkage block begins, else 0. The first unit of every device's 8 units begins a block, and a block holds 1 to 4 units of 256 variants. `unit_owner`: the index along var of the device that owns each unit's block, equal for all units of a block. For a unit of the device with index d along var it is (d + j) modulo the size of var, with 1 <= j <= 4. An owner holds at most 16 units and some owner holds exactly 16; the units of one device that belong to one owner are at most 4, and some device has exactly 4 for one owner.
All inputs are finite; a program needn't handle non-finite values.
Results may differ from the reference program's by a relative error of at most 0.0072.
Values may be sent and summed in bfloat16 or wider, within the bound.
A program may use at most 64 MiB of HBM per device.

```python
import math
import jax
import jax.numpy as jnp
from jax import lax

K = 128
UNIT = 256
BMAX = 4
REACH = 4
NS = 8192
NV = 131072
UNITS_DEV = 8
UNITS = 512
PAIR = 4
CAP = 16
SLOTS = 1024
N_VAR = 64


def layout(key):
    base = jax.random.fold_in(key, 9173)
    key_len, key_owner, key_score = jax.random.split(base, 3)
    shard_count = N_VAR
    per_shard = UNITS_DEV
    reach = REACH
    shard_ids = jnp.arange(shard_count, dtype=jnp.int32)
    hot_owner = jax.random.randint(key_owner, (), 0, shard_count)
    hot_gap = (hot_owner - shard_ids) % shard_count
    hot_shard = (hot_gap >= 1) & (hot_gap <= reach)
    lengths = jax.random.randint(key_len, (shard_count, per_shard), 1, PAIR + 1)
    lengths = lengths.at[:, 0].set(jnp.where(hot_shard, PAIR, lengths[:, 0]))
    block_ends = jnp.cumsum(lengths, axis=1)
    begins = block_ends - lengths
    positions = jnp.arange(per_shard, dtype=jnp.int32)
    starts_flag = jnp.any(begins[:, :, None] == positions[None, None, :], axis=1)
    begin_at = lax.cummax(jnp.where(starts_flag, positions[None, :], 0), axis=1)
    block_later = lax.cummin(jnp.where(starts_flag, positions[None, :], per_shard), axis=1, reverse=True)
    block_follow = jnp.concatenate([block_later[:, 1:], jnp.full((shard_count, 1), per_shard, jnp.int32)], axis=1)
    block_len = block_follow - begin_at

    def visit_unit(carried, column):
        group_fill, group_index = carried
        flag_now, length_now = column
        fresh_group = flag_now & (group_fill + length_now > PAIR)
        group_index = jnp.where(fresh_group, group_index + 1, group_index)
        group_fill = jnp.where(flag_now, jnp.where(fresh_group, length_now, group_fill + length_now), group_fill)
        return ((group_fill, group_index), group_index)
    start_state = (jnp.full((shard_count,), PAIR, jnp.int32), jnp.full((shard_count,), -1, jnp.int32))
    final_state, groups = lax.scan(visit_unit, start_state, (starts_flag.T, block_len.T))
    groups = groups.T
    reach_ids = jnp.arange(reach, dtype=jnp.int32)
    scores = jax.random.randint(key_score, (shard_count, reach), 0, 1024) * reach + reach_ids[None, :]
    forced = hot_shard[:, None] & (reach_ids[None, :] + 1 == hot_gap[:, None])
    scores = jnp.where(forced, -1, scores)
    order = jnp.argsort(scores, axis=1, stable=True).astype(jnp.int32)
    group_pick = jnp.clip(groups, 0, reach - 1)
    gaps = jnp.take_along_axis(order, group_pick, axis=1) + 1
    owners_out = ((shard_ids[:, None] + gaps) % shard_count).reshape(-1).astype(jnp.int32)
    return (starts_flag.astype(jnp.int32).reshape(-1), owners_out)


def draw_block_start(key, part):
    return layout(key)[0]


def draw_unit_owner(key, part):
    return layout(key)[1]


def strengthened(values, key, source, target, shards_of, factor):
    owner, partner = [(jnp.arange(values.shape[position]) // (values.shape[position] // shards_of)).reshape([-1 if axis == position else 1 for axis in range(values.ndim)]) for position in (source, target)]
    chosen = jax.random.permutation(key, shards_of)[partner]
    strong = (owner == chosen) | (owner == (partner + shards_of // 2) % shards_of)
    return jnp.where(strong, factor * values, values)


def block_levels(stream_key, extent, shards, low, top_value):
    factor_of = 1.0
    for axis_at, blocks in shards:
        heights = jax.random.uniform(jax.random.fold_in(jax.random.fold_in(stream_key, 6), axis_at), (blocks,), jnp.float32, low / len(shards), top_value / len(shards))
        factor_of = factor_of * jnp.repeat(jnp.exp(heights), extent[axis_at] // blocks).reshape((-1,) + (1,) * (len(extent) - 1 - axis_at))
    return factor_of


def noise(rng, dims, deviation, most, pieces=(), kind=jnp.bfloat16):
    array = jax.random.normal(rng, dims, jnp.float32) * deviation
    if len(pieces) > 0:
        array = block_levels(rng, dims, pieces, -0.22, 0.18) * array
    return jnp.clip(array, min=-most, max=most).astype(kind)


def noise_with(rng, extent, scale, most, shards, heavy, kind=jnp.bfloat16):
    drawn = scale * jax.random.normal(rng, extent, jnp.float32)
    if shards:
        drawn = drawn * block_levels(rng, extent, shards, -0.22, 0.18)
    return jnp.clip(strengthened(drawn, jax.random.fold_in(rng, 3), *heavy), -most, most).astype(kind)


def setup_inputs(seed: int = 0) -> dict:
    keys = jax.random.split(jax.random.key(seed), 9)
    dosage = noise_with(keys[0], (NS, NV), 1.0, 16.0, ((0, 4), (1, 64)), (1, 0, 64, 4.0))
    traits = noise(keys[1], (NS, K), 1.0, 6.0, ((0, 256),), jnp.float32)
    coef_now = noise(keys[2], (SLOTS, UNIT, K), 1.0, 6.0, ((0, 64), (1, 4)), jnp.float32)
    coef_prev = noise(keys[3], (SLOTS, UNIT, K), 1.0, 6.0, ((0, 64), (1, 4)), jnp.float32)
    block_inverse = noise(keys[4], (SLOTS, UNIT, BMAX, UNIT), (BMAX * UNIT) ** -0.5, 0.1875, ((0, 64), (1, 4)))
    penalty = jnp.clip(jnp.exp(jax.random.uniform(keys[5], (K,), jnp.float32, math.log(0.05), math.log(0.5))), 0.05, 0.5)
    block_start = draw_block_start(jax.random.fold_in(keys[8], 71), 0)
    unit_owner = draw_unit_owner(jax.random.fold_in(keys[8], 71), 0)
    return dict(dosage=dosage, traits=traits, coef_now=coef_now, coef_prev=coef_prev, block_inverse=block_inverse, penalty=penalty, block_start=block_start, unit_owner=unit_owner)


MOMENTA = (0.4, 0.55)

def unit_tables(block_start, unit_owner, per_device, owners):
    unit_count = block_start.shape[0]
    unit_ids = jnp.arange(unit_count, dtype=jnp.int32)
    shard_of = unit_ids // per_device
    owner_hot = (unit_owner[:, None] == jnp.arange(owners, dtype=jnp.int32)[None, :]).astype(jnp.int32)
    running = jnp.cumsum(owner_hot, axis=0) - owner_hot
    slot_index = lax.optimization_barrier(jnp.sum(running * owner_hot, axis=1))
    first_unit = shard_of * per_device
    before_shard = lax.optimization_barrier(jnp.sum(running[first_unit] * owner_hot, axis=1))
    pair_place = slot_index - before_shard
    block_begin = lax.cummax(jnp.where(block_start == 1, unit_ids, 0), axis=0)
    block_later = lax.cummin(jnp.where(block_start == 1, unit_ids, unit_count), axis=0, reverse=True)
    block_follow = jnp.concatenate([block_later[1:], jnp.full((1,), unit_count, jnp.int32)])
    block_length = block_follow - block_begin
    offset = unit_ids - block_begin
    return (shard_of, slot_index, pair_place, offset, block_length)

def soft_shrink(stepped, penalty):
    return jnp.sign(stepped) * jnp.maximum(jnp.abs(stepped) - penalty, 0.0)

def reference(dosage, traits, coef_now, coef_prev, block_inverse, penalty, block_start, unit_owner):
    shard_of, slot_index, pair_place, offset, block_length = unit_tables(block_start, unit_owner, UNITS_DEV, N_VAR)
    global_slot = (unit_owner * CAP + slot_index).astype(jnp.int32)
    inv_scale = 1.0 / math.sqrt(NV)
    grad_scale = 0.5 / math.sqrt(NS)
    current, previous = (coef_now, coef_prev)
    residual = traits
    for momentum in MOMENTA:
        point = current + momentum * (current - previous)
        unit_point = point[global_slot]
        values = unit_point.reshape(NV, K).astype(jnp.bfloat16)
        predicted = jnp.dot(dosage, values, preferred_element_type=jnp.float32) * inv_scale
        residual = predicted - traits
        residual_b = residual.astype(jnp.bfloat16)
        gradient = lax.dot_general(dosage, residual_b, (((0,), (0,)), ((), ())), preferred_element_type=jnp.float32) * grad_scale
        grad_b = gradient.astype(jnp.bfloat16).reshape(UNITS, UNIT, K)

        def direction_of(unit_at):
            block_first = unit_at - offset[unit_at]
            members = jnp.clip(block_first + jnp.arange(BMAX, dtype=jnp.int32), 0, UNITS - 1)
            live_flag = jnp.arange(BMAX, dtype=jnp.int32) < block_length[unit_at]
            block_grad = jnp.where(live_flag[:, None, None], grad_b[members].astype(jnp.float32), jnp.float32(0.0))
            panel_rows = block_inverse[global_slot[unit_at]].astype(jnp.float32)
            return jnp.einsum('rqc,qck->rk', panel_rows, block_grad)
        direction = lax.map(direction_of, jnp.arange(UNITS, dtype=jnp.int32))
        updated_units = soft_shrink(unit_point - direction, penalty)
        updated = jnp.zeros((SLOTS, UNIT, K), jnp.float32).at[global_slot].set(updated_units)
        previous, current = (current, updated)
    return (current, residual)
```

```python
import functools
import math

import jax
import jax.numpy as jnp
from jax import lax
from jax.experimental import pallas as pl
from jax.experimental.pallas import tpu as pltpu
from jax.sharding import PartitionSpec as P

MESH = pl.DeviceIdType.MESH
BF = jnp.bfloat16
F32 = jnp.float32
NZ, NX, NC = 8, 4, 2
NSAMP = 4
NVAR = 64
REACH = 4
PAIR = 4
CAP = 16
UNITS = 8
ROWS = 64
K = 128
T_CODE, T_BEGIN, T_LEN, T_SEND, T_LOCAL, T_BASE, T_COUNT, T_START = 0, 16, 32, 48, 64, 72, 76, 80


def step_kernel(
    dos_hbm, traits, cnow, cprev, bi_hbm, pen, bstart, uown,
    coef_out, res_out,
    dos, bi, coef, pb, out_v, recv_v, vals, core_out, core_in, x_out, x_in, z_out, z_in,
    rsum, gath, rbt, gfull, gs, r_in, og, out_g, recv_g, whole, tab,
    load_sem, v_s, v_r, vy_s, vy_r, c_s, c_r, x_s, x_r, z_s, z_r,
    az_s, az_r, ax_s, ax_r, ac_s, ac_r, ry_s, ry_r, g_s, g_r, w_s, w_r,
):
    s = lax.axis_index("samp")
    v = lax.axis_index("var")
    c = lax.rem(v, NC)
    x = lax.rem(v // NC, NX)
    z = v // (NC * NX)
    inv_scale = 1.0 / math.sqrt(NVAR * UNITS * 256)
    grad_scale = 0.5 / math.sqrt(NSAMP * 2048)

    def at(zz, xx, cc):
        return (s, (zz * NX + xx) * NC + cc)

    def gap(g):
        return (s, lax.rem(v + g + NVAR, NVAR))

    def samp_at(d):
        return (lax.rem(s + d, NSAMP), v)

    def x_at(d):
        return at(z, lax.rem(x + d, NX), c)

    def z_at(e):
        return at(lax.rem(z + e, NZ), x, c)

    sibling = at(z, x, 1 - c)

    def remote(src, dst, ssem, rsem, device):
        return pltpu.make_async_remote_copy(
            src_ref=src, dst_ref=dst, send_sem=ssem, recv_sem=rsem,
            device_id=device, device_id_type=MESH,
        )

    def load_rows(i, carry):
        half, rest = i // (NX * NZ), lax.rem(i, NX * NZ)
        xx, zz = rest // NZ, lax.rem(rest, NZ)
        cc = jnp.where(half == 0, 1 - c, c)
        source = ((zz * NX + xx) * NC + cc) * 32
        pltpu.make_async_copy(
            dos_hbm.at[pl.ds(pl.multiple_of(source, 32), 32)],
            dos.at[pl.ds(pl.multiple_of(i * 32, 32), 32)],
            load_sem.at[0],
        ).start()
        return carry

    prev_copy = pltpu.make_async_copy(cprev, coef.at[0], load_sem.at[1])
    now_copy = pltpu.make_async_copy(cnow, coef.at[1], load_sem.at[2])
    bi_copy = pltpu.make_async_copy(bi_hbm, bi, load_sem.at[3])
    prev_copy.start()
    now_copy.start()
    lax.fori_loop(0, NC * NX * NZ, load_rows, 0)
    bi_copy.start()

    barrier = pltpu.get_barrier_semaphore()
    peers = (
        [gap(g) for g in range(1, REACH + 1)] + [gap(-g) for g in range(1, REACH + 1)]
        + [samp_at(d) for d in range(1, NSAMP)] + [x_at(d) for d in range(1, NX)]
        + [z_at(e) for e in range(1, NZ)] + [sibling]
    )
    for peer in peers:
        pl.semaphore_signal(barrier, inc=1, device_id=peer, device_id_type=MESH)

    homes = [lax.rem(v - g + NVAR, NVAR) for g in range(1, REACH + 1)]
    counts = []
    for g in range(REACH):
        count = jnp.int32(0)
        for k in range(UNITS):
            count += (uown[homes[g] * UNITS + k] == v).astype(jnp.int32)
        counts.append(count)
    bases = []
    for g in range(REACH):
        base = jnp.int32(0)
        for other in range(REACH):
            if other != g:
                base += jnp.where(homes[other] < homes[g], counts[other], 0)
        bases.append(base)
        tab[T_BASE + g] = base
    tab[T_COUNT] = counts[0] + counts[1] + counts[2] + counts[3]
    mine = [uown[v * UNITS + k] for k in range(UNITS)]
    for k in range(UNITS):
        place = jnp.int32(0)
        for other in range(k):
            place += (mine[other] == mine[k]).astype(jnp.int32)
        ahead = mine[k] - v
        ahead = jnp.where(ahead < 0, ahead + NVAR, ahead)
        tab[T_LOCAL + k] = jnp.clip((ahead - 1) * PAIR + place, 0, CAP - 1)

    def more_tables():
        codes = [tab[T_LOCAL + k] for k in range(UNITS)]
        for code in range(CAP):
            unit = jnp.int32(0)
            for k in range(UNITS):
                unit = jnp.where(codes[k] == code, k, unit)
            tab[T_SEND + code] = unit
        for g in range(REACH):
            rank = jnp.int32(0)
            flags = [jnp.int32(1) for _ in range(PAIR)]
            for k in range(UNITS):
                at_unit = homes[g] * UNITS + k
                hit = uown[at_unit] == v
                begins = bstart[at_unit]
                for p in range(PAIR):
                    flags[p] = jnp.where(hit & (rank == p), begins, flags[p])
                rank += hit.astype(jnp.int32)
            for p in range(PAIR):
                tab[T_START + g * PAIR + p] = flags[p]
        begin = jnp.int32(0)
        starts = []
        for i in range(CAP):
            code = jnp.int32(0)
            for g in range(REACH):
                inside = (bases[g] <= i) & (i < bases[g] + counts[g])
                code = jnp.where(inside, g * PAIR + i - bases[g], code)
            code = jnp.clip(code, 0, CAP - 1)
            tab[T_CODE + i] = code
            live = i < tab[T_COUNT]
            first = (tab[T_START + code] == 1) | jnp.logical_not(live)
            starts.append(first)
            begin = jnp.where(first, i, begin)
            tab[T_BEGIN + i] = begin
        follow = jnp.int32(CAP)
        for i in reversed(range(CAP)):
            tab[T_LEN + i] = follow - tab[T_BEGIN + i]
            follow = jnp.where(starts[i], i, follow)

    prev_copy.wait()
    now_copy.wait()
    pl.semaphore_wait(barrier, len(peers))

    def tile(k, block):
        rows = dos[pl.ds(pl.multiple_of(block * 256, 256), 256), :]
        return inv_scale * jnp.dot(
            rows, vals[k].reshape(UNITS * 256, K), preferred_element_type=F32
        )

    def one_step(k, carry):
        momentum = jnp.where(k == 0, jnp.float32(0.4), jnp.float32(0.55))

        def to_point(i, carry):
            now = coef[k + 1, i]
            pb[i] = (now + momentum * (now - coef[k, i])).astype(BF)
            return carry

        lax.fori_loop(0, CAP, to_point, 0)
        sends = []
        for g in range(REACH):
            base = tab[T_BASE + g]
            for p in range(PAIR):
                out_v[k, g, p] = pb[jnp.minimum(base + p, CAP - 1)]
            copy = remote(
                out_v.at[k, g], recv_v.at[k, pl.ds(g * PAIR, PAIR)],
                v_s.at[k, g], v_r.at[k, g], gap(-(g + 1)),
            )
            copy.start()
            sends.append(copy)

        @pl.when(k == 0)
        def _():
            more_tables()

        for copy in sends:
            copy.wait_recv()
        for u in range(UNITS):
            vals[k, u, s] = recv_v[k, tab[T_LOCAL + u]]
        copies = []
        for d in (2, 1, 3):
            copy = remote(
                vals.at[k, :, s], vals.at[k, :, s], vy_s.at[k, d - 1], vy_r.at[k, d - 1], samp_at(d)
            )
            copy.start()
            copies.append(copy)
        sends += copies

        @pl.when(k == 0)
        def _():
            pltpu.make_async_copy(dos_hbm, dos, load_sem.at[0]).wait()
            bi_copy.wait()

        for copy in copies:
            copy.wait_recv()

        def core_copy(xx):
            return remote(
                core_out.at[k, xx], core_in.at[k, xx], c_s.at[k, xx], c_r.at[k, xx], sibling
            )

        def for_sibling(d, carry):
            xx = lax.rem(x + d, NX)
            core_out[k, xx] = tile(k, xx).astype(BF)
            core_copy(xx).start()
            return carry

        lax.fori_loop(1, NX + 1, for_sibling, 0)

        def x_copy(d):
            return remote(
                x_out.at[k, d - 1], x_in.at[k, d - 1], x_s.at[k, d - 1], x_r.at[k, d - 1], x_at(d)
            )

        def for_x(d, carry):
            xx = lax.rem(x + d, NX)
            mine_part = tile(k, NX + xx)
            core_copy(xx).wait_recv()
            total = mine_part + core_in[k, xx].astype(F32)

            @pl.when(d < NX)
            def _():
                x_out[k, d - 1] = total.astype(BF)
                x_copy(d).start()

            @pl.when(d == NX)
            def _():
                rsum[...] = total

            return carry

        lax.fori_loop(1, NX + 1, for_x, 0)
        for d in range(1, NX):
            x_copy(d).wait_recv()
        total = rsum[...]
        for d in range(1, NX):
            total += x_in[k, d - 1].astype(F32)
        rsum[...] = total
        z_out[k] = total.astype(BF)
        copies = []
        for e in range(1, NZ):
            there = lax.rem(z + e, NZ)
            copy = remote(
                z_out.at[k, pl.ds(pl.multiple_of(there * 32, 32), 32)], z_in.at[k, e - 1],
                z_s.at[k, e - 1], z_r.at[k, e - 1], z_at(e),
            )
            copy.start()
            copies.append(copy)
        sends += copies
        for copy in copies:
            copy.wait_recv()
        residual = rsum[pl.ds(pl.multiple_of(z * 32, 32), 32), :]
        for e in range(1, NZ):
            residual += z_in[k, e - 1].astype(F32)
        residual -= traits[...]
        res_out[...] = residual

        gath[k, 1, x, z] = residual.astype(BF)
        copies = []
        for e in range(1, NZ):
            copy = remote(
                gath.at[k, 1, x, z], gath.at[k, 1, x, z],
                az_s.at[k, e - 1], az_r.at[k, e - 1], z_at(e),
            )
            copy.start()
            copies.append(copy)
        sends += copies
        for copy in copies:
            copy.wait_recv()
        x_copies = []
        for d in (2, 1, 3):
            copy = remote(
                gath.at[k, 1, x], gath.at[k, 1, x],
                ax_s.at[k, d - 1], ax_r.at[k, d - 1], x_at(d),
            )
            copy.start()
            x_copies.append(copy)
        sends += x_copies
        last = []
        for d, arrived in ((0, None), (1, x_copies[1]), (3, x_copies[2]), (2, x_copies[0])):
            if arrived is not None:
                arrived.wait_recv()
            xx = lax.rem(x - d + NX, NX)
            copy = remote(
                gath.at[k, 1, xx], gath.at[k, 0, xx], ac_s.at[k, d], ac_r.at[k, d], sibling
            )
            copy.start()
            last.append(copy)
        sends += last
        for copy in last:
            copy.wait_recv()

        rbt[...] = gath[k].reshape(NC * NX * NZ * 32, K).astype(F32).T.astype(BF)

        def r_copy(piece, d):
            return remote(
                gs.at[k, piece, lax.rem(s + d, NSAMP)], r_in.at[k, piece, d - 1],
                ry_s.at[k, piece, d - 1], ry_r.at[k, piece, d - 1], samp_at(d),
            )

        def grad_piece(piece, carry):
            def grad_unit(uu, carry):
                first = (piece * PAIR + uu) * 256
                part = jnp.dot(
                    rbt[...], dos[:, pl.ds(pl.multiple_of(first, 256), 256)],
                    preferred_element_type=F32,
                )
                part = (grad_scale * part.T).reshape(NSAMP, ROWS, K)
                gs[k, piece, :, uu] = part.astype(BF)
                gfull[piece, uu] = part
                return carry

            lax.fori_loop(0, PAIR, grad_unit, 0)
            for d in (2, 1, 3):
                r_copy(piece, d).start()
            return carry

        lax.fori_loop(0, 2, grad_piece, 0)

        def sum_piece(piece, carry):
            for d in (1, 3, 2):
                r_copy(piece, d).wait_recv()
            for uu in range(PAIR):
                total = gfull[piece, uu, s]
                for d in range(1, NSAMP):
                    total += r_in[k, piece, d - 1, uu].astype(F32)
                og[piece * PAIR + uu] = total.astype(BF)
            return carry

        lax.fori_loop(0, 2, sum_piece, 0)
        copies = []
        for g in range(REACH):
            for p in range(PAIR):
                out_g[k, g, p] = og[tab[T_SEND + g * PAIR + p]]
            copy = remote(
                out_g.at[k, g], recv_g.at[k, pl.ds(g * PAIR, PAIR)],
                g_s.at[k, g], g_r.at[k, g], gap(g + 1),
            )
            copy.start()
            copies.append(copy)
        sends += copies
        for copy in copies:
            copy.wait_recv()
        for i in range(CAP):
            whole[k, i, s] = recv_g[k, tab[T_CODE + i]]
        copies = []
        for d in (2, 1, 3):
            copy = remote(
                whole.at[k, :, s], whole.at[k, :, s], w_s.at[k, d - 1], w_r.at[k, d - 1], samp_at(d)
            )
            copy.start()
            copies.append(copy)
        sends += copies
        for copy in copies:
            copy.wait_recv()

        def update(i, carry):
            begin, length = tab[T_BEGIN + i], tab[T_LEN + i]
            direction = jnp.zeros((ROWS, K), F32)
            for q in range(PAIR):
                member = whole[k, jnp.clip(begin + q, 0, CAP - 1)].reshape(256, K)
                part = jnp.dot(
                    bi[i, :, q * 256 : (q + 1) * 256], member, preferred_element_type=F32
                )
                direction += jnp.where(q < length, part, 0.0)
            now = coef[k + 1, i]
            stepped = now + momentum * (now - coef[k, i]) - direction
            level = pen[...]
            updated = stepped - jnp.clip(stepped, -level, level)
            updated = jnp.where(i < tab[T_COUNT], updated, 0.0)
            coef[k + 2, i] = updated
            coef_out[i] = updated
            return carry

        lax.fori_loop(0, CAP, update, 0)
        for copy in sends:
            copy.wait_send()
        for xx in range(NX):
            core_copy(xx).wait_send()
        for d in range(1, NX):
            x_copy(d).wait_send()
        for piece in range(2):
            for d in range(1, NSAMP):
                r_copy(piece, d).wait_send()
        return carry

    lax.fori_loop(0, 2, one_step, 0)


def shards(dosage, traits, coef_now, coef_prev, block_inverse, penalty, block_start, unit_owner):
    panel = block_inverse.reshape(CAP, ROWS, PAIR * 256)
    vmem = pl.BlockSpec(memory_space=pltpu.VMEM)
    smem = pl.BlockSpec(memory_space=pltpu.SMEM)
    anywhere = pl.BlockSpec(memory_space=pl.ANY)
    dma = pltpu.SemaphoreType.DMA
    pairs = []
    for count in (REACH, 3, NX, 3, 7, 7, 3, NX):
        pairs += [dma((2, count))] * 2
    pairs += [dma((2, 2, 3))] * 2
    for count in (REACH, 3):
        pairs += [dma((2, count))] * 2
    return pl.pallas_call(
        step_kernel,
        out_shape=(
            jax.ShapeDtypeStruct((CAP, ROWS, K), F32),
            jax.ShapeDtypeStruct((32, K), F32),
        ),
        in_specs=[anywhere, vmem, anywhere, anywhere, anywhere, vmem, smem, smem],
        out_specs=(vmem, vmem),
        scratch_shapes=[
            pltpu.VMEM((2048, 2048), BF),
            pltpu.VMEM((CAP, ROWS, 1024), BF),
            pltpu.VMEM((4, CAP, ROWS, K), F32),
            pltpu.VMEM((CAP, ROWS, K), BF),
            pltpu.VMEM((2, REACH, PAIR, ROWS, K), BF),
            pltpu.VMEM((2, CAP, ROWS, K), BF),
            pltpu.VMEM((2, UNITS, NSAMP, ROWS, K), BF),
            pltpu.VMEM((2, NX, 256, K), BF),
            pltpu.VMEM((2, NX, 256, K), BF),
            pltpu.VMEM((2, 3, 256, K), BF),
            pltpu.VMEM((2, 3, 256, K), BF),
            pltpu.VMEM((2, 256, K), BF),
            pltpu.VMEM((2, 7, 32, K), BF),
            pltpu.VMEM((256, K), F32),
            pltpu.VMEM((2, NC, NX, NZ, 32, K), BF),
            pltpu.VMEM((K, 2048), BF),
            pltpu.VMEM((2, PAIR, NSAMP, ROWS, K), F32),
            pltpu.VMEM((2, 2, NSAMP, PAIR, ROWS, K), BF),
            pltpu.VMEM((2, 2, 3, PAIR, ROWS, K), BF),
            pltpu.VMEM((UNITS, ROWS, K), BF),
            pltpu.VMEM((2, REACH, PAIR, ROWS, K), BF),
            pltpu.VMEM((2, CAP, ROWS, K), BF),
            pltpu.VMEM((2, CAP, NSAMP, ROWS, K), BF),
            pltpu.SMEM((96,), jnp.int32),
            dma((4,)),
            *pairs,
        ],
        compiler_params=pltpu.CompilerParams(
            collective_id=0, has_side_effects=True, vmem_limit_bytes=48 * 1024 * 1024
        ),
    )(
        dosage, traits, coef_now, coef_prev, panel, penalty.reshape(1, K), block_start, unit_owner
    )


def solution(mesh):
    placed = (
        P("samp", "var"),
        P(("samp", "var"), None),
        P("var", "samp", None),
        P("var", "samp", None),
        P("var", "samp", None, None),
        P(),
        P(),
        P(),
    )
    return jax.shard_map(
        shards,
        mesh=mesh,
        in_specs=placed,
        out_specs=(P("var", "samp", None), P(("samp", "var"), None)),
        check_vma=False,
    )
```

```python
import functools
import math

import jax
import jax.numpy as jnp
from jax import lax
from jax.experimental import pallas as pl
from jax.experimental.pallas import tpu as pltpu
from jax.sharding import PartitionSpec as P

MESH = pl.DeviceIdType.MESH
BF = jnp.bfloat16
F32 = jnp.float32
NZ, NX, NC = 8, 4, 2
NSAMP = 4
NVAR = 64
REACH = 4
PAIR = 4
CAP = 16
UNITS = 8
ROWS = 64
K = 128
T_CODE, T_BEGIN, T_LEN, T_SEND, T_SLOT, T_LOCAL, T_COUNT = 0, 16, 32, 48, 64, 80, 88
MOMENTA = (0.4, 0.55)


def step_kernel(
    dos_hbm, traits, cnow, cprev, bi, pen, bstart, uown,
    coef_out, res_out,
    dos, panel, coef, point, out_v, recv_v, vals, core_out, core_in, x_out, x_in, z_out, z_in,
    part, rsum, gath, rbt, gfull, gs, r_in, og, out_g, whole, tab,
    load_sem, v_s, v_r, vy_s, vy_r, c_s, c_r, x_s, x_r, z_s, z_r,
    az_s, az_r, ax_s, ax_r, ac_s, ac_r, ry_s, ry_r, g_s, g_r, w_s, w_r, f_s, f_r,
):
    s = lax.axis_index("samp")
    v = lax.axis_index("var")
    c = lax.rem(v, NC)
    x = lax.rem(v // NC, NX)
    z = v // (NC * NX)
    inv_scale = 1.0 / math.sqrt(NVAR * UNITS * 256)
    grad_scale = 0.5 / math.sqrt(NSAMP * 2048)

    def at(zz, xx, cc):
        return (s, (zz * NX + xx) * NC + cc)

    gaps = {g: (s, lax.rem(v + g + NVAR, NVAR)) for g in range(-REACH, REACH + 1)}
    samps = [lax.rem(s + d, NSAMP) for d in range(NSAMP)]
    xs = [lax.rem(x + d, NX) for d in range(NX)]
    zs = [lax.rem(z + e, NZ) for e in range(NZ)]
    halves = [z // 4 * 4, (1 - z // 4) * 4]
    samp_at = [(samps[d], v) for d in range(NSAMP)]
    x_at = [at(z, xs[d], c) for d in range(NX)]
    z_at = [at(zs[e], x, c) for e in range(NZ)]
    half_at = [[at(halves[half] + lax.rem(z + j, 4), x, c) for j in range(4)] for half in range(2)]

    sibling = at(z, x, 1 - c)

    def remote(src, dst, ssem, rsem, device):
        return pltpu.make_async_remote_copy(
            src_ref=src, dst_ref=dst, send_sem=ssem, recv_sem=rsem,
            device_id=device, device_id_type=MESH,
        )

    def wait_arrived(ref, sem):
        remote(ref, ref, sem, sem, sibling).wait_recv()

    def wait_sent(ref, sem):
        remote(ref, ref, sem, sem, sibling).wait_send()

    load_copies = [
        pltpu.make_async_copy(
            dos_hbm.at[:, xx, cc], dos.at[half, xx], load_sem.at[half * NX + xx]
        )
        for half, cc in ((0, 1 - c), (1, c))
        for xx in range(NX)
    ]

    barrier = pltpu.get_barrier_semaphore()
    peers = (
        [gaps[g] for g in range(-REACH, REACH + 1) if g != 0]
        + samp_at[1:] + x_at[1:] + z_at[1:] + [sibling]
    )
    for peer in peers:
        pl.semaphore_signal(barrier, inc=1, device_id=peer, device_id_type=MESH)

    homes = [gaps[-g][1] for g in range(1, REACH + 1)]
    counts = []
    for g in range(REACH):
        count = jnp.int32(0)
        for k in range(UNITS):
            count += (uown[homes[g] * UNITS + k] == v).astype(jnp.int32)
        counts.append(count)
    bases = []
    for g in range(REACH):
        base = jnp.int32(0)
        for other in range(REACH):
            if other != g:
                base += jnp.where(homes[other] < homes[g], counts[other], 0)
        bases.append(base)
        for p in range(PAIR):
            tab[T_SLOT + g * PAIR + p] = jnp.minimum(base + p, CAP - 1)
    tab[T_COUNT] = counts[0] + counts[1] + counts[2] + counts[3]

    def more_tables():
        mine = [uown[v * UNITS + k] for k in range(UNITS)]
        codes = []
        for k in range(UNITS):
            place = jnp.int32(0)
            for other in range(k):
                place += (mine[other] == mine[k]).astype(jnp.int32)
            ahead = mine[k] - v
            ahead = jnp.where(ahead < 0, ahead + NVAR, ahead)
            codes.append(jnp.clip((ahead - 1) * PAIR + place, 0, CAP - 1))
            tab[T_LOCAL + k] = codes[k]
        for code in range(CAP):
            unit = jnp.int32(0)
            for k in range(UNITS):
                unit = jnp.where(codes[k] == code, k, unit)
            tab[T_SEND + code] = unit
        for g in range(REACH):
            rank = jnp.int32(0)
            flags = [jnp.int32(1) for _ in range(PAIR)]
            for k in range(UNITS):
                at_unit = homes[g] * UNITS + k
                hit = uown[at_unit] == v
                begins = bstart[at_unit]
                for p in range(PAIR):
                    flags[p] = jnp.where(hit & (rank == p), begins, flags[p])
                rank += hit.astype(jnp.int32)
            begin = jnp.int32(0)
            begin_of = []
            for p in range(PAIR):
                begin = jnp.where(flags[p] == 1, p, begin)
                begin_of.append(begin)
                tab[T_BEGIN + g * PAIR + p] = begin
            follow = jnp.int32(PAIR)
            for p in reversed(range(PAIR)):
                tab[T_LEN + g * PAIR + p] = follow - begin_of[p]
                follow = jnp.where(flags[p] == 1, p, follow)
        for i in range(CAP):
            code = jnp.int32(0)
            for g in range(REACH):
                inside = (bases[g] <= i) & (i < bases[g] + counts[g])
                code = jnp.where(inside, g * PAIR + i - bases[g], code)
            tab[T_CODE + i] = jnp.clip(code, 0, CAP - 1)

    def v_copy(k, g):
        here = pl.ds(g * PAIR, PAIR)
        return remote(
            out_v.at[k, here], recv_v.at[k, here], v_s.at[k], v_r.at[k], gaps[-(g + 1)]
        )

    for code in range(CAP):
        slot = tab[T_SLOT + code]
        now, before = cnow[slot], cprev[slot]
        coef[code] = now
        moved = now + MOMENTA[0] * (now - before)
        point[code] = moved
        out_v[0, code] = moved.astype(BF)
    pl.semaphore_wait(barrier, len(peers))
    for g in reversed(range(REACH)):
        v_copy(0, g).start()
    for copy in load_copies:
        copy.start()
    more_tables()

    def fill_panel(code, carry):
        slot, begin, length = tab[T_SLOT + code], tab[T_BEGIN + code], tab[T_LEN + code]
        for member in range(PAIR):
            q = member - begin
            block = bi[slot, jnp.clip(q, 0, PAIR - 1)]
            live = (q >= 0) & (q < length)
            panel[code, :, member * 256 : (member + 1) * 256] = jnp.where(live, block, zero)
        return carry

    zero = jnp.zeros((), BF)
    lax.fori_loop(0, CAP, fill_panel, 0)

    def product(k, block, half):
        columns = slice(half * 1024, (half + 1) * 1024)
        return jnp.dot(
            dos[block // NX, lax.rem(block, NX), :, :, columns].reshape(256, 1024),
            vals[k, half * PAIR : (half + 1) * PAIR].reshape(1024, K),
            preferred_element_type=F32,
        )

    def tile(k, block):
        return inv_scale * (part[block] + product(k, block, 1))

    def one_step(k, carry):
        wait_arrived(recv_v.at[k], v_r.at[k])
        for u in range(UNITS):
            vals[k, u, s] = recv_v[k, tab[T_LOCAL + u]]
        for half in range(2):
            here = vals.at[k, pl.ds(half * PAIR, PAIR), s]
            for d in (2, 1, 3):
                remote(here, here, vy_s.at[k], vy_r.at[k, half], samp_at[d]).start()

        @pl.when(k == 0)
        def _():
            for copy in load_copies:
                copy.wait()

        wait_arrived(x_in.at[k], vy_r.at[k, 0])

        def first_half(block, carry):
            part[block] = product(k, block, 0)
            return carry

        lax.fori_loop(0, 2 * NX, first_half, 0)
        wait_arrived(x_in.at[k], vy_r.at[k, 1])

        def core_copy(xx):
            return remote(
                core_out.at[k, xx], core_in.at[k, xx], c_s.at[k], c_r.at[k, xx], sibling
            )

        for d in (2, 1, 3, 0):
            core_out[k, xs[d]] = tile(k, xs[d]).astype(BF)
            core_copy(xs[d]).start()
        for d in (2, 1, 3, 0):
            mine_part = tile(k, NX + xs[d])
            core_copy(xs[d]).wait_recv()
            total = mine_part + core_in[k, xs[d]].astype(F32)
            if d:
                x_out[k, d - 1] = total.astype(BF)
                remote(
                    x_out.at[k, d - 1], x_in.at[k, d - 1], x_s.at[k], x_r.at[k], x_at[d]
                ).start()
        wait_arrived(x_in.at[k], x_r.at[k])
        for d in range(1, NX):
            total += x_in[k, d - 1].astype(F32)
        rsum[...] = total
        z_out[k] = total.astype(BF)
        for e in (4, 3, 5, 2, 6, 1, 7):
            there = pl.ds(pl.multiple_of(zs[e] * 32, 32), 32)
            remote(
                z_out.at[k, there], z_in.at[k, e - 1], z_s.at[k], z_r.at[k], z_at[e]
            ).start()
        residual = rsum[pl.ds(pl.multiple_of(z * 32, 32), 32), :] - traits[...]
        wait_arrived(z_in.at[k], z_r.at[k])
        for e in range(1, NZ):
            residual += z_in[k, e - 1].astype(F32)
        res_out[...] = residual

        gath[k, 1, x, z] = residual.astype(BF)
        mine_rows = gath.at[k, 1, x, z]
        for half, j in ((1, 0), (1, 1), (1, 3), (1, 2), (0, 2), (0, 1), (0, 3)):
            remote(
                mine_rows, mine_rows, az_s.at[k], az_r.at[k, half], half_at[half][j]
            ).start()

        def gath_x(half, d):
            here = gath.at[k, 1, x, pl.ds(halves[half], 4)]
            return remote(here, here, ax_s.at[k], ax_r.at[k, half, d], x_at[d])

        def gath_core(half, d):
            xx, here = xs[NX - d if d else 0], pl.ds(halves[half], 4)
            return remote(
                gath.at[k, 1, xx, here], gath.at[k, 0, xx, here], ac_s.at[k], ac_r.at[k], sibling
            )

        for half in range(2):
            wait_arrived(z_in.at[k, pl.ds(0, 3 + half)], az_r.at[k, half])
            for d in (2, 1, 3):
                gath_x(half, d).start()
            gath_core(half, 0).start()
        for half in range(2):
            for d in (1, 3, 2):
                gath_x(half, d).wait_recv()
                gath_core(half, d).start()
        wait_arrived(gath.at[k, 0], ac_r.at[k])

        rbt[...] = gath[k].reshape(NC * NX * NZ * 32, K).astype(F32).T.astype(BF)

        def grad_piece(piece, carry):
            def grad_unit(uu, carry):
                first = (piece * PAIR + uu) * 256
                grad = jnp.dot(
                    rbt[...],
                    dos[:, :, :, :, pl.ds(pl.multiple_of(first, 256), 256)].reshape(2048, 256),
                    preferred_element_type=F32,
                )
                grad = (grad_scale * grad.T).reshape(NSAMP, ROWS, K)
                gs[k, piece, :, uu] = grad.astype(BF)
                gfull[piece, uu] = grad
                return carry

            lax.fori_loop(0, PAIR, grad_unit, 0)
            for d in (2, 1, 3):
                remote(
                    gs.at[k, piece, samps[d]], r_in.at[k, piece, d - 1],
                    ry_s.at[k], ry_r.at[k, piece], samp_at[d],
                ).start()
            return carry

        lax.fori_loop(0, 2, grad_piece, 0)
        for piece in range(2):
            wait_arrived(r_in.at[k, piece], ry_r.at[k, piece])
            for uu in range(PAIR):
                total = gfull[piece, uu, s]
                for d in range(1, NSAMP):
                    total += r_in[k, piece, d - 1, uu].astype(F32)
                og[piece * PAIR + uu] = total.astype(BF)

        def g_copy(g):
            here = pl.ds(g * PAIR, PAIR)
            return remote(
                out_g.at[k, here], whole.at[k, here, s], g_s.at[k], g_r.at[k, g], gaps[g + 1]
            )

        for g in reversed(range(REACH)):
            for p in range(PAIR):
                out_g[k, g * PAIR + p] = og[tab[T_SEND + g * PAIR + p]]
            g_copy(g).start()
        for g in range(REACH):
            g_copy(g).wait_recv()
            here = whole.at[k, pl.ds(g * PAIR, PAIR), s]
            for d in (1, 3):
                remote(here, here, w_s.at[k], w_r.at[k, g], samp_at[d]).start()
        for g in range(REACH):
            wait_arrived(out_g.at[k, pl.ds(0, 2 * PAIR)], w_r.at[k, g])
            for d, first in ((1, 0), (3, PAIR // 2)):
                here = whole.at[k, pl.ds(g * PAIR + first, PAIR // 2), samps[NSAMP - d]]
                remote(here, here, f_s.at[k], f_r.at[k, g], samp_at[d]).start()

        level = pen[...]
        for g in range(REACH):
            wait_arrived(out_g.at[k, pl.ds(0, PAIR)], f_r.at[k, g])
            here = pl.ds(g * PAIR, PAIR)
            directions = jnp.dot(
                panel[here].reshape(PAIR * ROWS, PAIR * 256),
                whole[k, here].reshape(PAIR * 256, K),
                preferred_element_type=F32,
            ).reshape(PAIR, ROWS, K)
            for p in range(PAIR):
                code = g * PAIR + p
                stepped = point[code] - directions[p]
                updated = stepped - jnp.clip(stepped, -level, level)
                moved = updated + MOMENTA[1] * (updated - coef[code])
                coef[code] = updated
                point[code] = moved
                out_v[k + 1, code] = moved.astype(BF)

            @pl.when(k == 0)
            def _():
                v_copy(1, g).start()

        return carry

    lax.fori_loop(0, 2, one_step, 0)
    for i in range(CAP):
        coef_out[i] = jnp.where(i < tab[T_COUNT], coef[tab[T_CODE + i]], 0.0)
    for k in range(2):
        for ref, sem in (
            (recv_v, v_s), (r_in, vy_s), (core_out, c_s), (x_out, x_s), (z_in, z_s), (z_in, az_s),
            (x_out, ax_s), (core_out, ac_s), (r_in, ry_s), (out_g, g_s), (vals, w_s), (out_g, f_s),
        ):
            wait_sent(ref.at[k], sem.at[k])


def shards(dosage, traits, coef_now, coef_prev, block_inverse, penalty, block_start, unit_owner):
    panel = block_inverse.transpose(0, 2, 1, 3)
    vmem = pl.BlockSpec(memory_space=pltpu.VMEM)
    smem = pl.BlockSpec(memory_space=pltpu.SMEM)
    anywhere = pl.BlockSpec(memory_space=pl.ANY)
    dma = pltpu.SemaphoreType.DMA
    pairs = []
    for arrivals in (
        (2,), (2, 2), (2, NX), (2,), (2,), (2, 2), (2, 2, NX), (2,), (2, 2), (2, REACH),
        (2, REACH), (2, REACH),
    ):
        pairs += [dma((2,)), dma(arrivals)]
    return pl.pallas_call(
        step_kernel,
        out_shape=(
            jax.ShapeDtypeStruct((CAP, ROWS, K), F32),
            jax.ShapeDtypeStruct((32, K), F32),
        ),
        in_specs=[anywhere, vmem, vmem, vmem, vmem, vmem, smem, smem],
        out_specs=(vmem, vmem),
        scratch_shapes=[
            pltpu.VMEM((NC, NX, NZ, 32, 2048), BF),
            pltpu.VMEM((CAP, ROWS, PAIR * 256), BF),
            pltpu.VMEM((CAP, ROWS, K), F32),
            pltpu.VMEM((CAP, ROWS, K), F32),
            pltpu.VMEM((3, CAP, ROWS, K), BF),
            pltpu.VMEM((2, CAP, ROWS, K), BF),
            pltpu.VMEM((2, UNITS, NSAMP, ROWS, K), BF),
            pltpu.VMEM((2, NX, 256, K), BF),
            pltpu.VMEM((2, NX, 256, K), BF),
            pltpu.VMEM((2, 3, 256, K), BF),
            pltpu.VMEM((2, 3, 256, K), BF),
            pltpu.VMEM((2, 256, K), BF),
            pltpu.VMEM((2, 7, 32, K), BF),
            pltpu.VMEM((NC * NX, 256, K), F32),
            pltpu.VMEM((256, K), F32),
            pltpu.VMEM((2, NC, NX, NZ, 32, K), BF),
            pltpu.VMEM((K, 2048), BF),
            pltpu.VMEM((2, PAIR, NSAMP, ROWS, K), F32),
            pltpu.VMEM((2, 2, NSAMP, PAIR, ROWS, K), BF),
            pltpu.VMEM((2, 2, 3, PAIR, ROWS, K), BF),
            pltpu.VMEM((UNITS, ROWS, K), BF),
            pltpu.VMEM((2, CAP, ROWS, K), BF),
            pltpu.VMEM((2, CAP, NSAMP, ROWS, K), BF),
            pltpu.SMEM((96,), jnp.int32),
            dma((8,)),
            *pairs,
        ],
        compiler_params=pltpu.CompilerParams(
            collective_id=0, has_side_effects=True, vmem_limit_bytes=48 * 1024 * 1024
        ),
    )(
        dosage.reshape(NZ, NX, NC, 32, UNITS * 256), traits, coef_now, coef_prev, panel, penalty.reshape(1, K), block_start, unit_owner
    )


def solution(mesh):
    placed = (
        P("samp", "var"),
        P(("samp", "var"), None),
        P("var", "samp", None),
        P("var", "samp", None),
        P("var", "samp", None, None),
        P(),
        P(),
        P(),
    )
    return jax.shard_map(
        shards,
        mesh=mesh,
        in_specs=placed,
        out_specs=(P("var", "samp", None), P(("samp", "var"), None)),
        check_vma=False,
    )
```
